512 devices in a mesh: samp: 32 (over x, z), blk: 16 (over y, core).
Axes of the slice: x: 4, y: 8, z: 8, core: 2. Of those that a mesh axis runs over, the one named last changes fastest.
Arguments:
- dosages: int32 [49152, 8192], P('samp', 'blk'), may hold values from 0 to 2, as said below
- new_dosages: int32 [49152, 2048], P('samp', 'blk'), may hold values from 0 to 2, as said below
- traits: float32 [64, 49152], P(None, 'samp'), may hold values from -40 to 40
- shrink: float32 [5], replicated, may hold values from 0.5 to 5
Outputs:
- residual: float32 [5, 64, 49152], P(None, 'blk', 'samp')
- scores: float32 [5, 64, 2048], P(None, None, 'blk')
The draws below stay inside these ranges and needn't reach their ends.
Inputs may be any that keep to these rules, and one draw needn't show every extreme that they name: `dosages`: codes of haplotype pairs, with linkage along neighbouring variants. `new_dosages`: codes of haplotype pairs, with linkage along neighbouring variants.
All inputs are finite; a program needn't handle non-finite values.
Results may differ from the reference program's by a relative error of at most 0.0053.
Values may be sent and summed in bfloat16 or wider, within the bound.
No kernel may reach another device: no remote copies, remote signals or barrier semaphores. Data moves between devices by JAX's collectives and lax.ppermute only.
A program may use at most 64 MiB of HBM per device.

```python
import math
import jax
import jax.numpy as jnp
from jax import lax

VB = 512
TRAITS = 64
RIDGE = 5
CHEB = 3
SAMPLES = 49152
BLOCKS = 16
VARIANTS = 8192
NEW_TOTAL = 2048


def haplotype_codes(base_key, row_count, column_count):
    level_key, column_key, start_key = jax.random.split(base_key, 3)
    allele_levels = jax.random.randint(level_key, (column_count,), 1, 8)
    column_keys = jax.random.split(column_key, column_count)
    bit_shape = (2 * row_count,)
    start_bits = jax.random.randint(start_key, bit_shape, 0, 2)

    def advance(previous, scan_inputs):
        one_key, allele_level = scan_inputs
        copy_key, fresh_key = jax.random.split(one_key)
        copy_mask = jax.random.randint(copy_key, bit_shape, 0, 4) < 3
        fresh_bits = (jax.random.randint(fresh_key, bit_shape, 0, 8) < allele_level).astype(jnp.int32)
        current = jnp.where(copy_mask, previous, fresh_bits)
        return (current, current)
    unused, haplotypes = lax.scan(advance, start_bits, (column_keys, allele_levels))
    code_matrix = haplotypes[:, :row_count] + haplotypes[:, row_count:]
    return code_matrix.T.astype(jnp.int32)


def draw_dosages(key, part):
    return haplotype_codes(jax.random.fold_in(key, 11), SAMPLES, VARIANTS)


def draw_new_dosages(key, part):
    return haplotype_codes(jax.random.fold_in(key, 12), SAMPLES, NEW_TOTAL)


def draw_traits(key, part):
    code_matrix = haplotype_codes(jax.random.fold_in(key, 11), SAMPLES, VARIANTS)
    effect = jax.random.normal(jax.random.fold_in(key, 13), (VARIANTS, TRAITS), jnp.float32)
    effect = effect * jnp.sqrt(0.5 / (2.6 * VARIANTS))
    genetic = jnp.dot(code_matrix.astype(jnp.float32) - 1.0, effect)
    noise_key = jax.random.fold_in(key, 14)
    noise = 0.7 * jax.random.truncated_normal(noise_key, -4.0, 4.0, (SAMPLES, TRAITS), jnp.float32)
    trait_scale = jnp.ones((TRAITS,), jnp.float32)
    values = (genetic + noise) * trait_scale[None, :]
    return jnp.clip(values, -40.0, 40.0).T


def setup_inputs(seed: int = 0) -> dict:
    streams_of = jax.random.split(jax.random.key(seed), 5)
    return {
        "dosages": draw_dosages(jax.random.fold_in(streams_of[4], 71), 0),
        "new_dosages": draw_new_dosages(jax.random.fold_in(streams_of[4], 71), 0),
        "traits": draw_traits(jax.random.fold_in(streams_of[4], 71), 0),
        "shrink": jnp.clip(jnp.exp(jax.random.uniform(streams_of[3], (RIDGE,), jnp.float32, math.log(0.5), math.log(5.0))), 0.5, 5.0),
    }


def standardize(code_block, count):
    values = code_block.astype(jnp.float32)
    column_mean = lax.optimization_barrier(jnp.sum(values, axis=0)) / count
    column_var = lax.optimization_barrier(jnp.sum(values * values, axis=0)) / count - column_mean * column_mean
    inverse = 1.0 / jnp.sqrt(column_var + 1e-05)
    return ((values - column_mean) * inverse).astype(jnp.bfloat16)

def chebyshev(rhs_cols, apply_fn, centre, half_width, sweeps):
    sig_ratio = centre / half_width
    factor = 1.0 / sig_ratio
    direction = rhs_cols / centre
    iterate = jnp.zeros_like(rhs_cols)
    remain = rhs_cols
    for sweep_index in range(sweeps):
        iterate = iterate + direction
        if sweep_index + 1 < sweeps:
            remain = remain - apply_fn(direction)
            factor_next = 1.0 / (2.0 * sig_ratio - factor)
            direction = factor_next * factor * direction + 2.0 * factor_next / half_width * remain
            factor = factor_next
    return iterate

def reference(dosages, new_dosages, traits, shrink):
    count = float(dosages.shape[0])
    trait_bf = traits.astype(jnp.bfloat16)
    lam_cols = jnp.repeat(shrink, TRAITS)

    def block_term(total, block_id):
        codes = lax.dynamic_slice_in_dim(dosages, block_id * VB, VB, 1)
        standard = standardize(codes, count)
        gram = jnp.dot(standard.T, standard, preferred_element_type=jnp.float32)
        cross = jnp.dot(standard.T, trait_bf.T, preferred_element_type=jnp.float32)
        bound = jnp.max(lax.optimization_barrier(jnp.sum(jnp.abs(gram), axis=0))) / count
        rhs_cols = jnp.tile(cross / count, (1, RIDGE))

        def apply_fn(direction):
            return jnp.dot(gram, direction, precision=lax.Precision.HIGHEST) / count + lam_cols * direction
        centre = lam_cols + bound / 2.0
        half_width = bound / 2.0 + jnp.zeros_like(lam_cols)
        weights = chebyshev(rhs_cols, apply_fn, centre, half_width, CHEB).astype(jnp.bfloat16)
        pred = jnp.dot(weights.T, standard.T, preferred_element_type=jnp.float32)
        return (total + pred, None)
    start_total = jnp.zeros((RIDGE * TRAITS, dosages.shape[0]), jnp.float32)
    pred, unused = lax.scan(block_term, start_total, jnp.arange(BLOCKS, dtype=jnp.int32))
    residual = traits[None, :, :] - pred.reshape(RIDGE, TRAITS, dosages.shape[0])
    res_bf = residual.astype(jnp.bfloat16).reshape(RIDGE * TRAITS, dosages.shape[0])
    fresh = standardize(new_dosages, count)
    raw = jnp.dot(res_bf, fresh, preferred_element_type=jnp.float32)
    res_float = res_bf.astype(jnp.float32)
    sum_sq = lax.optimization_barrier(jnp.sum(res_float * res_float, axis=1))
    scores = raw / jnp.sqrt(count * (sum_sq / count + 1e-05))[:, None]
    return (residual, scores.reshape(RIDGE, TRAITS, new_dosages.shape[1]))
```

```python
import jax
import jax.numpy as jnp
from jax import lax
from jax.sharding import Mesh, PartitionSpec as P

RIDGE = 5
SAMP = ("x", "z")
BLK = ("y", "core")
FACTORS = {32: (4, 8), 16: (8, 2), 4: (2, 2)}
EPS = 1e-05
F32 = jnp.float32
BF16 = jnp.bfloat16


def dot(a, b, contract, precision=None):
    return lax.dot_general(
        a, b, (contract, ((), ())), precision=precision, preferred_element_type=F32
    )


def rounded(values):
    return lax.reduce_precision(values, 8, 7)


def column_stats(shifted_sum, shifted_sq, count):
    mean = (shifted_sum + count) / count
    var = (shifted_sq + 2.0 * shifted_sum + count) / count - mean * mean
    return mean, 1.0 / jnp.sqrt(var + EPS)


def scaled(codes, mean, inv):
    return ((codes.astype(F32) - mean) * inv).astype(BF16)


def affine(shifted_sum, shifted_sq, mean, inv, count):
    low, mid, high = (rounded((code - mean) * inv) for code in (0.0, 1.0, 2.0))
    n_low = (shifted_sq - shifted_sum) * 0.5
    n_high = (shifted_sq + shifted_sum) * 0.5
    n_mid = count - shifted_sq
    value_mean = (n_low * low + n_mid * mid + n_high * high) / count
    pairs = n_low * n_mid + n_mid * n_high + 4.0 * n_low * n_high
    slopes = (
        n_low * n_mid * (mid - low)
        + n_mid * n_high * (high - mid)
        + 2.0 * n_low * n_high * (high - low)
    )
    slope = jnp.where(pairs > 0.0, slopes / jnp.maximum(pairs, 1.0), inv)
    square = (n_low * low * low + n_mid * mid * mid + n_high * high * high) / count
    return value_mean, slope, square


def chebyshev_coefficients(lam, bound):
    centre = lam + bound / 2.0
    half = bound / 2.0
    sig = centre / half
    q0 = 1.0 / sig
    d0 = 1.0 / centre
    r1a, r1b = 1.0 - lam * d0, -d0
    q1 = 1.0 / (2.0 * sig - q0)
    step = 2.0 * q1 / half
    d1a, d1b = q1 * q0 * d0 + step * r1a, step * r1b
    r2a = r1a - lam * d1a
    r2b = r1b - d1a - lam * d1b
    r2c = -d1b
    q2 = 1.0 / (2.0 * sig - q1)
    step = 2.0 * q2 / half
    d2a, d2b, d2c = q2 * q1 * d1a + step * r2a, q2 * q1 * d1b + step * r2b, step * r2c
    return d0 + d1a + d2a, d1b + d2b, d2c


def shards(dosages, new_dosages, traits, shrink):
    rows, width = dosages.shape
    fresh_width = new_dosages.shape[1]
    trait_count = traits.shape[0]
    samp, blk = lax.axis_size(SAMP), lax.axis_size(BLK)
    depth, cores, zs = lax.axis_size("y"), lax.axis_size("core"), lax.axis_size("z")
    count = float(rows * samp)
    half_width = width // 2
    share_rows = half_width // samp
    share = trait_count // blk
    columns = RIDGE * trait_count

    codes = (dosages - 1).astype(BF16)
    codes_f = (dosages - 1).astype(F32)
    new_f = (new_dosages - 1).astype(F32)
    trait_bf = traits.astype(BF16)
    parts = (
        jnp.sum(codes_f, axis=0),
        jnp.sum(codes_f * codes_f, axis=0),
        jnp.sum(new_f, axis=0),
        jnp.sum(new_f * new_f, axis=0),
        jnp.sum(trait_bf.astype(F32), axis=1),
    )
    sizes = [p.shape[0] for p in parts]
    slots = share_rows * 256
    sums = jnp.pad(jnp.concatenate(parts), (0, slots - sum(sizes))).reshape(share_rows, 256)
    first, second = codes[:, :half_width], codes[:, half_width:]
    over_rows = ((0,), (0,))
    gram_top = dot(first, codes, over_rows)
    gram_low = dot(second, second, over_rows)
    cross = dot(codes, trait_bf, ((0,), (1,)))
    wide = 3 * half_width
    payload = jnp.concatenate(
        [gram_top, gram_low, cross[:half_width], cross[half_width:]], axis=1
    ).reshape(samp, share_rows, wide + 2 * trait_count)
    payload = jnp.concatenate(
        [payload, jnp.broadcast_to(sums[None], (samp, share_rows, 256))], axis=2
    )
    chunk = jnp.sum(lax.all_to_all(payload, SAMP, 0, 0, tiled=True), axis=0)

    totals = chunk[:, wide + 2 * trait_count :].reshape(slots)
    pieces, at = [], 0
    for size in sizes:
        pieces.append(totals[at : at + size])
        at += size
    code_sum, code_sq, new_sum, new_sq, trait_sum = pieces
    mean, inv = column_stats(code_sum, code_sq, count)
    value_mean, slope, square = affine(code_sum, code_sq, mean, inv, count)

    start = lax.axis_index(SAMP) * share_rows

    def own(vector, offset):
        return lax.dynamic_slice(vector, (start + offset,), (share_rows,))[:, None]

    def centred(product, offset, column_from):
        sums_i, slope_i, value_i = (own(v, offset) for v in (code_sum, slope, value_mean))
        out = slope_i * slope[None, column_from:] * (
            product / count - (sums_i / count) * (code_sum[None, column_from:] / count)
        )
        out = out + value_i * value_mean[None, column_from:]
        row = start + offset + lax.broadcasted_iota(jnp.int32, out.shape, 0)
        column = column_from + lax.broadcasted_iota(jnp.int32, out.shape, 1)
        return jnp.where(row == column, 0.0, out)

    def centred_cross(product, offset):
        sums_i, slope_i, value_i = (own(v, offset) for v in (code_sum, slope, value_mean))
        trait_mean = trait_sum[None, :] / count
        return slope_i * (product / count - (sums_i / count) * trait_mean) + value_i * trait_mean

    rhs_rows = jnp.concatenate(
        [
            centred_cross(chunk[:, wide : wide + trait_count], 0),
            centred_cross(chunk[:, wide + trait_count : wide + 2 * trait_count], half_width),
        ],
        axis=1,
    )
    rhs_high = rounded(rhs_rows)
    own_rows = jnp.concatenate(
        [
            centred(chunk[:, :width], 0, 0),
            centred(chunk[:, width:wide], half_width, half_width),
            rhs_high,
            rhs_rows - rhs_high,
        ],
        axis=1,
    ).astype(BF16)
    every = lax.all_to_all(
        jnp.broadcast_to(own_rows[None], (samp, *own_rows.shape)), SAMP, 0, 0, tiled=True
    ).reshape(half_width, own_rows.shape[1])

    top_left, top_right = every[:, :half_width], every[:, half_width:width]
    low_right = every[:, width:wide]
    gram = jnp.concatenate(
        [
            jnp.concatenate([top_left, top_right], axis=1),
            jnp.concatenate([top_right.T, low_right], axis=1),
        ],
        axis=0,
    )
    bound = jnp.max(jnp.sum(jnp.abs(gram.astype(F32)), axis=0) + square)
    rhs_parts = every[:, wide:].reshape(half_width, 2, 2, trait_count)
    rhs_parts = rhs_parts.transpose(1, 3, 2, 0).reshape(2 * trait_count, width)

    def apply_gram(high, low, whole):
        out = dot(jnp.concatenate([high, low], axis=0), gram, ((1,), (0,)))
        return out[:trait_count] + out[trait_count:] + square[None, :] * whole

    high, low = rhs_parts[:trait_count], rhs_parts[trait_count:]
    rhs = high.astype(F32) + low.astype(F32)
    once = apply_gram(high, low, rhs)
    once_high = rounded(once)
    twice = apply_gram(once_high.astype(BF16), (once - once_high).astype(BF16), once)
    coefficients = chebyshev_coefficients(shrink, bound)

    row = lax.broadcasted_iota(jnp.int32, (columns, 3 * trait_count), 0)
    column = lax.broadcasted_iota(jnp.int32, (columns, 3 * trait_count), 1)
    side, in_side = row // (columns // cores), row % (columns // cores)
    place, in_place = in_side // (RIDGE * share), in_side % (RIDGE * share)
    ridge, in_share = in_place // share, in_place % share
    core = lax.rem(lax.axis_index("core") + 1 + side, cores)
    trait = (place * cores + core) * share + in_share
    mixing = jnp.zeros((columns, 3 * trait_count), F32)
    for power in range(3):
        for r in range(RIDGE):
            mixing = jnp.where(
                (ridge == r) & (column == trait + power * trait_count),
                coefficients[power][r],
                mixing,
            )
    weights = dot(
        mixing,
        jnp.concatenate([rhs, once, twice], axis=0),
        ((1,), (0,)),
        lax.Precision.HIGHEST,
    ).astype(BF16)

    standard = scaled(dosages, mean, inv)
    new_mean, new_inv = column_stats(new_sum, new_sq, count)
    fresh = scaled(new_dosages, new_mean, new_inv)

    half_columns = columns // cores
    along = ((1,), (1,))
    sent = dot(weights[:half_columns], standard, along).astype(BF16)
    kept = dot(weights[half_columns:], standard, along)
    arrived = lax.ppermute(sent, "core", [(0, 1), (1, 0)])
    paired = (kept + arrived.astype(F32)).astype(BF16).reshape(depth, RIDGE * share, rows)
    summed = lax.all_to_all(paired, "y", 0, 0, tiled=True)
    pred = jnp.sum(summed.astype(F32), axis=0).reshape(RIDGE, share, rows)

    own_traits = lax.dynamic_slice_in_dim(traits, lax.axis_index(BLK) * share, share, 0)
    residual = own_traits[None] - pred
    res_bf = lax.all_gather(
        residual.astype(BF16).reshape(RIDGE * share, rows), BLK, axis=0, tiled=True
    )
    raw_part = dot(res_bf, fresh, ((1,), (0,)))
    res_float = res_bf.astype(F32)
    squares = jnp.sum(res_float * res_float, axis=1).reshape(zs, 1, columns // zs)
    squares = jnp.pad(squares, ((0, 0), (0, 7), (0, fresh_width - columns // zs)))
    ends = jnp.concatenate([raw_part.reshape(zs, columns // zs, fresh_width), squares], axis=1)
    ends = jnp.sum(lax.all_to_all(ends, "z", 0, 0, tiled=True), axis=0)
    ends = lax.psum(ends, "x")
    raw, sum_sq = ends[: columns // zs], ends[columns // zs, : columns // zs]
    scores = raw / jnp.sqrt(count * (sum_sq / count + EPS))[:, None]
    scores = lax.all_to_all(
        jnp.broadcast_to(scores[None], (zs, *scores.shape)), "z", 0, 0, tiled=True
    )
    scores = scores.reshape(blk, RIDGE, share, fresh_width).transpose(1, 0, 2, 3)
    return residual, scores.reshape(RIDGE, trait_count, fresh_width)


def solution(mesh):
    samp, blk = FACTORS[mesh.shape["samp"]], FACTORS[mesh.shape["blk"]]
    grid = Mesh(mesh.devices.reshape(*samp, *blk), SAMP + BLK)
    return jax.shard_map(
        shards,
        mesh=grid,
        in_specs=(P(SAMP, BLK), P(SAMP, BLK), P(None, SAMP), P()),
        out_specs=(P(None, BLK, SAMP), P(None, None, BLK)),
        check_vma=False,
    )
```

```python
import functools

import jax
import jax.numpy as jnp
from jax import lax
from jax.experimental import pallas as pl
from jax.experimental.pallas import tpu as pltpu
from jax.sharding import Mesh, PartitionSpec as P


RIDGE = 5
SAMP = ("x", "z")
BLK = ("y", "core")
FACTORS = {32: (4, 8), 16: (8, 2), 4: (2, 2)}
EPS = 1e-05
TILE = 128
SUMS = 3 * TILE
F32 = jnp.float32
BF16 = jnp.bfloat16
EXACT = lax.Precision.HIGHEST


def dot(a, b, contract, precision=None):
    return lax.dot_general(
        a, b, (contract, ((), ())), precision=precision, preferred_element_type=F32
    )


def rounded(values):
    return lax.reduce_precision(values, 8, 7)


def split(values):
    high = values.astype(BF16)
    return high, (values - high.astype(F32)).astype(BF16)


def gram_tiles(width, samp):
    at = 0
    for block_row in range(width // TILE):
        for block_column in range(block_row, width // TILE):
            for group in range(TILE // 8):
                yield block_row * TILE + 8 * group, block_column * TILE, at % samp, at // samp
                at += 1


def cross_tiles(trait_count, width, samp):
    at = 0
    for group in range(trait_count // 8):
        for block in range(width // TILE):
            yield 8 * group, block * TILE, at % samp, at // samp
            at += 1


def places(width, trait_count, samp):
    blocks = width // TILE
    gram = blocks * (blocks + 1) // 2 * (TILE // 8) // samp
    return gram, trait_count // 8 * blocks // samp


def products_kernel(samp, rows, dosages, new_dosages, traits, out, gram, cross, sums, new_sums, trait_sums):
    width, trait_count = dosages.shape[1], traits.shape[0]
    half = width // 2
    step = pl.program_id(0)

    @pl.when(step == 0)
    def _():
        for ref in (gram, cross, sums, new_sums, trait_sums):
            ref[...] = jnp.zeros_like(ref)

    codes_f = (dosages[...] - 1).astype(F32)
    codes = codes_f.astype(BF16)
    new_f = (new_dosages[...] - 1).astype(F32)
    trait_bf = traits[...].astype(BF16)
    ones = jnp.ones((8, codes.shape[0]), BF16)
    over_rows = ((0,), (0,))
    gram[:half, :] += dot(codes[:, :half], codes, over_rows)
    gram[half:, half:] += dot(codes[:, half:], codes[:, half:], over_rows)
    cross[...] += dot(trait_bf, codes, ((1,), (0,)))
    sums[:8] += dot(ones, codes, ((1,), (0,)))
    sums[8:] += dot(ones, (codes_f * codes_f).astype(BF16), ((1,), (0,)))
    new_sums[:8] += dot(ones, new_f.astype(BF16), ((1,), (0,)))
    new_sums[8:] += dot(ones, (new_f * new_f).astype(BF16), ((1,), (0,)))
    trait_sums[...] += dot(ones, trait_bf, ((1,), (1,)))

    @pl.when(step == pl.num_programs(0) - 1)
    def _():
        local = sums[:8]
        shift = 1.0 / (8.0 * rows)
        gram[...] = gram[...] - dot(local, local, over_rows, EXACT) * shift
        cross[...] = cross[...] - dot(trait_sums[...], local, over_rows, EXACT) * shift
        gram_places, cross_places = places(width, trait_count, samp)
        for row, column, owner, place in gram_tiles(width, samp):
            out[owner, :, place * TILE : (place + 1) * TILE] = gram[
                row : row + 8, column : column + TILE
            ].astype(BF16)
        for row, column, owner, place in cross_tiles(trait_count, width, samp):
            high, low = split(cross[row : row + 8, column : column + TILE])
            at = (gram_places + place) * TILE
            out[owner, :, at : at + TILE] = high
            at += cross_places * TILE
            out[owner, :, at : at + TILE] = low
        lines = []
        for block in range(4):
            line = [sums[0:1, block * TILE : (block + 1) * TILE], sums[8:9, block * TILE : (block + 1) * TILE]]
            if block == 0:
                line.append(new_sums[0:1])
            elif block == 1:
                line.append(new_sums[8:9])
            elif block == 2:
                spare = jnp.zeros((1, TILE - trait_count), F32)
                line.append(jnp.concatenate([trait_sums[0:1], spare], axis=1))
            else:
                line.append(jnp.zeros((1, TILE), F32))
            lines.append(jnp.concatenate(line, axis=1))
        values = jnp.concatenate(lines, axis=0)
        kept = rounded_in_kernel(values)
        packed = jnp.concatenate([kept, values - kept], axis=0).astype(BF16)
        at = (gram_places + 2 * cross_places) * TILE
        out[:, :, at:] = jnp.broadcast_to(packed[None], (samp, 8, SUMS))


def rounded_in_kernel(values):
    return values.astype(BF16).astype(F32)


def products(dosages, new_dosages, traits, samp):
    rows, width = dosages.shape
    fresh_width, trait_count = new_dosages.shape[1], traits.shape[0]
    gram_places, cross_places = places(width, trait_count, samp)
    lanes = (gram_places + 2 * cross_places) * TILE + SUMS
    step = min(512, rows)
    return pl.pallas_call(
        functools.partial(products_kernel, samp, rows),
        grid=(rows // step,),
        in_specs=[
            pl.BlockSpec((step, width), lambda i: (i, 0)),
            pl.BlockSpec((step, fresh_width), lambda i: (i, 0)),
            pl.BlockSpec((trait_count, step), lambda i: (0, i)),
        ],
        out_specs=pl.BlockSpec((samp, 8, lanes), lambda i: (0, 0, 0)),
        out_shape=jax.ShapeDtypeStruct((samp, 8, lanes), BF16),
        scratch_shapes=[
            pltpu.VMEM((width, width), F32),
            pltpu.VMEM((trait_count, width), F32),
            pltpu.VMEM((16, width), F32),
            pltpu.VMEM((16, fresh_width), F32),
            pltpu.VMEM((8, trait_count), F32),
        ],
        name="products",
    )(dosages, new_dosages, traits)


def owner_kernel(gram_lanes, cross_lanes, received, out, sums):
    samp = received.shape[0]
    values = received[:, :, gram_lanes + 2 * cross_lanes :].astype(F32)
    sums[...] = values[:, :4] + values[:, 4:]
    total = jnp.sum(received[:, :, : gram_lanes + 2 * cross_lanes].astype(F32), axis=0)
    cross = total[:, gram_lanes : gram_lanes + cross_lanes] + total[:, gram_lanes + cross_lanes :]
    high = rounded_in_kernel(cross)
    own = jnp.concatenate([total[:, :gram_lanes], high, cross - high], axis=1).astype(BF16)
    out[...] = jnp.broadcast_to(own[None], (samp, *own.shape))


def owner(received, gram_lanes, cross_lanes):
    lanes = gram_lanes + 2 * cross_lanes
    return pl.pallas_call(
        functools.partial(owner_kernel, gram_lanes, cross_lanes),
        out_shape=[
            jax.ShapeDtypeStruct((*received.shape[:2], lanes), BF16),
            jax.ShapeDtypeStruct((received.shape[0], 4, SUMS), F32),
        ],
        name="owner",
    )(received)


def column_stats(shifted_sum, shifted_sq, count):
    mean = (shifted_sum + count) / count
    var = (shifted_sq + 2.0 * shifted_sum + count) / count - mean * mean
    return mean, 1.0 / jnp.sqrt(var + EPS)


def scaled(codes, mean, inv):
    return ((codes.astype(F32) - mean) * inv).astype(BF16)


def affine(shifted_sum, shifted_sq, mean, inv, count):
    low, mid, high = (rounded((code - mean) * inv) for code in (0.0, 1.0, 2.0))
    n_low = (shifted_sq - shifted_sum) * 0.5
    n_high = (shifted_sq + shifted_sum) * 0.5
    n_mid = count - shifted_sq
    value_mean = (n_low * low + n_mid * mid + n_high * high) / count
    pairs = n_low * n_mid + n_mid * n_high + 4.0 * n_low * n_high
    slopes = (
        n_low * n_mid * (mid - low)
        + n_mid * n_high * (high - mid)
        + 2.0 * n_low * n_high * (high - low)
    )
    slope = jnp.where(pairs > 0.0, slopes / jnp.maximum(pairs, 1.0), inv)
    square = (n_low * low * low + n_mid * mid * mid + n_high * high * high) / count
    return value_mean, slope, square


def chebyshev_coefficients(lam, bound):
    centre = lam + bound / 2.0
    half = bound / 2.0
    sig = centre / half
    q0 = 1.0 / sig
    d0 = 1.0 / centre
    r1a, r1b = 1.0 - lam * d0, -d0
    q1 = 1.0 / (2.0 * sig - q0)
    step = 2.0 * q1 / half
    d1a, d1b = q1 * q0 * d0 + step * r1a, step * r1b
    r2a = r1a - lam * d1a
    r2b = r1b - d1a - lam * d1b
    r2c = -d1b
    q2 = 1.0 / (2.0 * sig - q1)
    step = 2.0 * q2 / half
    d2a, d2b, d2c = q2 * q1 * d1a + step * r2a, q2 * q1 * d1b + step * r2b, step * r2c
    return d0 + d1a + d2a, d1b + d2b, d2c


def ridge_kernel(count, depth, padded, core, lam, every, between, rhs_shift, slope, square, standard,
                 sent, kept, gram, cross, weights):
    samp = every.shape[0]
    width, trait_count = gram.shape[0], cross.shape[0]
    gram_places, cross_places = places(width, trait_count, samp)
    for row, column, owned, place in gram_tiles(width, samp):
        gram[row : row + 8, column : column + TILE] = every[
            owned, :, place * TILE : (place + 1) * TILE
        ].astype(F32)
    for block_row in range(width // TILE):
        for block_column in range(block_row + 1, width // TILE):
            gram[block_column * TILE : (block_column + 1) * TILE, block_row * TILE : (block_row + 1) * TILE] = gram[
                block_row * TILE : (block_row + 1) * TILE, block_column * TILE : (block_column + 1) * TILE
            ].T
    for row, column, owned, place in cross_tiles(trait_count, width, samp):
        at = (gram_places + place) * TILE
        low = at + cross_places * TILE
        cross[row : row + 8, column : column + TILE] = every[owned, :, at : at + TILE].astype(F32) + every[
            owned, :, low : low + TILE
        ].astype(F32)
    scale = slope[...]
    diagonal = square[...]
    matrix = gram[...] * (1.0 / count) + between[...]
    same = lax.broadcasted_iota(jnp.int32, matrix.shape, 0) == lax.broadcasted_iota(jnp.int32, matrix.shape, 1)
    matrix = jnp.where(same, 0.0, matrix)
    rhs = cross[...] * (1.0 / count) * scale + rhs_shift[...]

    def apply_gram(values):
        return dot(values * scale, matrix, ((1,), (0,)), EXACT) * scale + diagonal * values

    once = apply_gram(rhs)
    twice = apply_gram(once)
    eight = jnp.broadcast_to(scale, (8, width))
    column_sums = dot(eight, jnp.abs(matrix), ((1,), (0,)), EXACT)[0:1] * scale + diagonal
    bound = jnp.max(column_sums, axis=1, keepdims=True)
    for r in range(RIDGE):
        coefficients = chebyshev_coefficients(lam[r : r + 1, :], bound)
        a, b, c = (
            jnp.broadcast_to(jnp.concatenate([v] * (width // TILE), axis=1), (8, width))
            for v in coefficients
        )
        for y in range(depth):
            at, to = slice(8 * y, 8 * y + 8), 8 * (RIDGE * y + r)
            weights[to : to + 8] = a * rhs[at] + b * once[at] + c * twice[at]
    whole = weights[...].astype(BF16)

    def chosen(which):
        parts = []
        for y in range(depth):
            i = lax.broadcasted_iota(jnp.int32, (padded, whole.shape[0]), 0)
            j = lax.broadcasted_iota(jnp.int32, (padded, whole.shape[0]), 1)
            wanted = 8 * RIDGE * y + 2 * i - (i & 3) + 4 * which
            parts.append(((j == wanted) & (i < 4 * RIDGE)).astype(F32))
        select = jnp.concatenate(parts, axis=0).astype(BF16)
        return dot(select, whole, ((1,), (0,))).astype(BF16)

    mine = core[0]
    along = ((1,), (1,))
    sent[...] = dot(chosen(1 - mine), standard[...], along).astype(BF16)
    kept[...] = dot(chosen(mine), standard[...], along)


def ridge(core, lam, every, between, rhs_shift, slope, square, standard, count, depth, padded):
    rows, width = standard.shape
    trait_count = rhs_shift.shape[0]
    vmem = pl.BlockSpec(memory_space=pltpu.VMEM)
    return pl.pallas_call(
        functools.partial(ridge_kernel, count, depth, padded),
        in_specs=[pl.BlockSpec(memory_space=pltpu.SMEM)] + [vmem] * 7,
        out_specs=[vmem, vmem],
        out_shape=[
            jax.ShapeDtypeStruct((depth * padded, rows), BF16),
            jax.ShapeDtypeStruct((depth * padded, rows), F32),
        ],
        scratch_shapes=[
            pltpu.VMEM((width, width), F32),
            pltpu.VMEM((trait_count, width), F32),
            pltpu.VMEM((RIDGE * trait_count, width), F32),
        ],
        name="ridge",
    )(core, lam, every, between, rhs_shift, slope, square, standard)


def from_sums(sums, dosages, new_dosages, trait_count, count):
    (rows, width), samp = dosages.shape, sums.shape[0]
    code_sums = sums[:, :, :TILE].reshape(samp, width)
    trait_sums = sums[:, 2, 2 * TILE : 2 * TILE + trait_count]
    totals = jnp.sum(sums, axis=0)
    code_sum, code_sq = totals[:, :TILE].reshape(width), totals[:, TILE : 2 * TILE].reshape(width)
    new_sum, new_sq = totals[0, 2 * TILE :], totals[1, 2 * TILE :]
    trait_sum = totals[2, 2 * TILE : 2 * TILE + trait_count]
    mean, inv = column_stats(code_sum, code_sq, count)
    value_mean, slope, square = affine(code_sum, code_sq, mean, inv, count)
    new_mean, new_inv = column_stats(new_sum, new_sq, count)
    standard = scaled(dosages, mean, inv)
    fresh = scaled(new_dosages, new_mean, new_inv)
    code_shift = code_sums / rows - code_sum / count
    trait_shift = trait_sums / rows - trait_sum / count
    over_parts = ((0,), (0,))
    between = dot(code_shift, code_shift, over_parts, EXACT) * (1.0 / samp)
    rhs_shift = dot(trait_shift, code_shift, over_parts, EXACT) * (slope[None] * (1.0 / samp))
    rhs_shift = rhs_shift + (trait_sum / count)[:, None] * value_mean[None]
    return standard, fresh, between, rhs_shift, slope, square


def shards(dosages, new_dosages, traits, shrink):
    rows, width = dosages.shape
    fresh_width = new_dosages.shape[1]
    trait_count = traits.shape[0]
    samp, blk = lax.axis_size(SAMP), lax.axis_size(BLK)
    depth, xs, zs = lax.axis_size("y"), lax.axis_size("x"), lax.axis_size("z")
    count = float(rows * samp)
    share = trait_count // blk
    used = RIDGE * share
    padded = (used // 8 + 1) * 8
    gram_places, cross_places = places(width, trait_count, samp)

    payload = products(dosages, new_dosages, traits, samp)
    received = lax.all_to_all(payload, SAMP, 0, 0, tiled=True)
    own_rows, sums = owner(received, gram_places * TILE, cross_places * TILE)
    every = lax.all_to_all(own_rows, SAMP, 0, 0, tiled=True)
    prepared = from_sums(sums, dosages, new_dosages, trait_count, count)
    standard, fresh, between, rhs_shift, slope, square = prepared

    core = lax.axis_index("core").astype(jnp.int32).reshape(1)
    lam = jnp.broadcast_to(jnp.pad(shrink, (0, 3), constant_values=1.0)[:, None], (8, TILE))
    sent, kept = ridge(
        core, lam, every, between, rhs_shift, slope[None], square[None], standard, count, depth, padded
    )

    arrived = lax.ppermute(sent, "core", [(0, 1), (1, 0)])
    paired = (kept + arrived.astype(F32)).astype(BF16).reshape(depth, padded, rows)
    summed = lax.all_to_all(paired, "y", 0, 0, tiled=True)
    pred = jnp.sum(summed.astype(F32), axis=0)[:used].reshape(RIDGE, share, rows)

    own_traits = lax.dynamic_slice_in_dim(traits, lax.axis_index(BLK) * share, share, 0)
    residual = own_traits[None] - pred
    res_bf = lax.all_gather(residual.astype(BF16).reshape(1, used, rows), BLK, axis=0, tiled=True)
    res_bf = res_bf.reshape(blk * used, rows)
    raw_part = dot(res_bf, fresh, ((1,), (0,))).reshape(blk, used, fresh_width)
    res_float = res_bf.astype(F32)
    squares = jnp.sum(res_float * res_float, axis=1).reshape(blk, 1, used)
    squares = jnp.pad(squares, ((0, 0), (0, padded - used - 1), (0, fresh_width - used)))
    ends = jnp.concatenate([raw_part, squares], axis=1)
    ends = lax.all_to_all(ends.reshape(zs, blk // zs * padded, fresh_width), "z", 0, 0, tiled=True)
    ends = jnp.sum(ends, axis=0)
    ends = lax.all_to_all(jnp.broadcast_to(ends[None], (xs, *ends.shape)), "x", 0, 0, tiled=True)
    ends = jnp.sum(ends, axis=0).reshape(blk // zs, padded, fresh_width)
    sum_sq = ends[:, used, :used]
    scores = ends[:, :used] / jnp.sqrt(count * (sum_sq / count + EPS))[:, :, None]
    scores = scores.reshape(blk // zs * used, fresh_width)
    scores = lax.all_to_all(
        jnp.broadcast_to(scores[None], (zs, *scores.shape)), "z", 0, 0, tiled=True
    )
    scores = scores.reshape(blk, RIDGE, share, fresh_width).transpose(1, 0, 2, 3)
    return residual, scores.reshape(RIDGE, trait_count, fresh_width)


def solution(mesh):
    samp, blk = FACTORS[mesh.shape["samp"]], FACTORS[mesh.shape["blk"]]
    grid = Mesh(mesh.devices.reshape(*samp, *blk), SAMP + BLK)
    return jax.shard_map(
        shards,
        mesh=grid,
        in_specs=(P(SAMP, BLK), P(SAMP, BLK), P(None, SAMP), P()),
        out_specs=(P(None, BLK, SAMP), P(None, None, BLK)),
        check_vma=False,
    )
```

```python
import functools

import jax
import jax.numpy as jnp
from jax import lax
from jax.experimental import pallas as pl
from jax.experimental.pallas import tpu as pltpu
from jax.sharding import Mesh, PartitionSpec as P


RIDGE = 5
SAMP = ("x", "z")
BLK = ("y", "core")
FACTORS = {32: (4, 8), 16: (8, 2), 4: (2, 2)}
EPS = 1e-05
TILE = 128
SUMS = 3 * TILE
F32 = jnp.float32
BF16 = jnp.bfloat16
LIMIT = 30 << 20
EXACT = lax.Precision.HIGHEST


def dot(a, b, contract, precision=None):
    return lax.dot_general(
        a, b, (contract, ((), ())), precision=precision, preferred_element_type=F32
    )


def rounded(values):
    return lax.reduce_precision(values, 8, 7)


def split(values):
    high = values.astype(BF16)
    return high, (values - high.astype(F32)).astype(BF16)


def gram_tiles(width, samp):
    at = 0
    for block_row in range(width // TILE):
        for block_column in range(block_row, width // TILE):
            for group in range(TILE // 8):
                yield block_row * TILE + 8 * group, block_column * TILE, at % samp, at // samp
                at += 1


def cross_tiles(trait_count, width, samp):
    at = 0
    for group in range(trait_count // 8):
        for block in range(width // TILE):
            yield 8 * group, block * TILE, at % samp, at // samp
            at += 1


def places(width, trait_count, samp):
    blocks = width // TILE
    gram = blocks * (blocks + 1) // 2 * (TILE // 8) // samp
    return gram, trait_count // 8 * blocks // samp


def products_kernel(samp, rows, dosages, new_dosages, traits, out, gram, cross, sums, new_sums, trait_sums):
    width, trait_count = dosages.shape[1], traits.shape[0]
    half = width // 2
    step = pl.program_id(0)

    @pl.when(step == 0)
    def _():
        for ref in (gram, cross, sums, new_sums, trait_sums):
            ref[...] = jnp.zeros_like(ref)

    codes_f = (dosages[...] - 1).astype(F32)
    codes = codes_f.astype(BF16)
    new_f = (new_dosages[...] - 1).astype(F32)
    trait_bf = traits[...].astype(BF16)
    ones = jnp.ones((8, codes.shape[0]), BF16)
    over_rows = ((0,), (0,))
    gram[:half, :] += dot(codes[:, :half], codes, over_rows)
    gram[half:, half:] += dot(codes[:, half:], codes[:, half:], over_rows)
    cross[...] += dot(trait_bf, codes, ((1,), (0,)))
    sums[:8] += dot(ones, codes, ((1,), (0,)))
    sums[8:] += dot(ones, (codes_f * codes_f).astype(BF16), ((1,), (0,)))
    new_sums[:8] += dot(ones, new_f.astype(BF16), ((1,), (0,)))
    new_sums[8:] += dot(ones, (new_f * new_f).astype(BF16), ((1,), (0,)))
    trait_sums[...] += dot(ones, trait_bf, ((1,), (1,)))

    @pl.when(step == pl.num_programs(0) - 1)
    def _():
        local = sums[:8]
        shift = 1.0 / (8.0 * rows)
        gram[...] = gram[...] - dot(local, local, over_rows, EXACT) * shift
        cross[...] = cross[...] - dot(trait_sums[...], local, over_rows, EXACT) * shift
        gram_places, cross_places = places(width, trait_count, samp)
        for row, column, owner, place in gram_tiles(width, samp):
            out[owner, :, place * TILE : (place + 1) * TILE] = gram[
                row : row + 8, column : column + TILE
            ].astype(BF16)
        for row, column, owner, place in cross_tiles(trait_count, width, samp):
            high, low = split(cross[row : row + 8, column : column + TILE])
            at = (gram_places + place) * TILE
            out[owner, :, at : at + TILE] = high
            at += cross_places * TILE
            out[owner, :, at : at + TILE] = low
        lines = []
        for block in range(4):
            line = [sums[0:1, block * TILE : (block + 1) * TILE], sums[8:9, block * TILE : (block + 1) * TILE]]
            if block == 0:
                line.append(new_sums[0:1])
            elif block == 1:
                line.append(new_sums[8:9])
            elif block == 2:
                spare = jnp.zeros((1, TILE - trait_count), F32)
                line.append(jnp.concatenate([trait_sums[0:1], spare], axis=1))
            else:
                line.append(jnp.zeros((1, TILE), F32))
            lines.append(jnp.concatenate(line, axis=1))
        values = jnp.concatenate(lines, axis=0)
        kept = rounded_in_kernel(values)
        packed = jnp.concatenate([kept, values - kept], axis=0).astype(BF16)
        at = (gram_places + 2 * cross_places) * TILE
        out[:, :, at:] = jnp.broadcast_to(packed[None], (samp, 8, SUMS))


def rounded_in_kernel(values):
    return values.astype(BF16).astype(F32)


def products(dosages, new_dosages, traits, samp):
    rows, width = dosages.shape
    fresh_width, trait_count = new_dosages.shape[1], traits.shape[0]
    gram_places, cross_places = places(width, trait_count, samp)
    lanes = (gram_places + 2 * cross_places) * TILE + SUMS
    step = min(512, rows)
    return pl.pallas_call(
        functools.partial(products_kernel, samp, rows),
        grid=(rows // step,),
        in_specs=[
            pl.BlockSpec((step, width), lambda i: (i, 0)),
            pl.BlockSpec((step, fresh_width), lambda i: (i, 0)),
            pl.BlockSpec((trait_count, step), lambda i: (0, i)),
        ],
        out_specs=pl.BlockSpec((samp, 8, lanes), lambda i: (0, 0, 0)),
        out_shape=jax.ShapeDtypeStruct((samp, 8, lanes), BF16),
        scratch_shapes=[
            pltpu.VMEM((width, width), F32),
            pltpu.VMEM((trait_count, width), F32),
            pltpu.VMEM((16, width), F32),
            pltpu.VMEM((16, fresh_width), F32),
            pltpu.VMEM((8, trait_count), F32),
        ],
        name="products",
    )(dosages, new_dosages, traits)


def owner_kernel(gram_lanes, cross_lanes, received, out, sums):
    samp = received.shape[0]
    values = received[:, :, gram_lanes + 2 * cross_lanes :].astype(F32)
    sums[...] = values[:, :4] + values[:, 4:]
    total = jnp.sum(received[:, :, : gram_lanes + 2 * cross_lanes].astype(F32), axis=0)
    cross = total[:, gram_lanes : gram_lanes + cross_lanes] + total[:, gram_lanes + cross_lanes :]
    high = rounded_in_kernel(cross)
    own = jnp.concatenate([total[:, :gram_lanes], high, cross - high], axis=1).astype(BF16)
    out[...] = jnp.broadcast_to(own[None], (samp, *own.shape))


def owner(received, gram_lanes, cross_lanes):
    lanes = gram_lanes + 2 * cross_lanes
    return pl.pallas_call(
        functools.partial(owner_kernel, gram_lanes, cross_lanes),
        out_shape=[
            jax.ShapeDtypeStruct((*received.shape[:2], lanes), BF16),
            jax.ShapeDtypeStruct((received.shape[0], 4, SUMS), F32),
        ],
        compiler_params=pltpu.CompilerParams(vmem_limit_bytes=LIMIT),
        name="owner",
    )(received)


def column_stats(shifted_sum, shifted_sq, count):
    mean = (shifted_sum + count) / count
    var = (shifted_sq + 2.0 * shifted_sum + count) / count - mean * mean
    return mean, 1.0 / jnp.sqrt(var + EPS)


def scaled(codes, mean, inv):
    return ((codes.astype(F32) - mean) * inv).astype(BF16)


def affine(shifted_sum, shifted_sq, mean, inv, count):
    low, mid, high = (rounded((code - mean) * inv) for code in (0.0, 1.0, 2.0))
    n_low = (shifted_sq - shifted_sum) * 0.5
    n_high = (shifted_sq + shifted_sum) * 0.5
    n_mid = count - shifted_sq
    value_mean = (n_low * low + n_mid * mid + n_high * high) / count
    pairs = n_low * n_mid + n_mid * n_high + 4.0 * n_low * n_high
    slopes = (
        n_low * n_mid * (mid - low)
        + n_mid * n_high * (high - mid)
        + 2.0 * n_low * n_high * (high - low)
    )
    slope = jnp.where(pairs > 0.0, slopes / jnp.maximum(pairs, 1.0), inv)
    square = (n_low * low * low + n_mid * mid * mid + n_high * high * high) / count
    return value_mean, slope, square


def chebyshev_coefficients(lam, bound):
    centre = lam + bound / 2.0
    half = bound / 2.0
    sig = centre / half
    q0 = 1.0 / sig
    d0 = 1.0 / centre
    r1a, r1b = 1.0 - lam * d0, -d0
    q1 = 1.0 / (2.0 * sig - q0)
    step = 2.0 * q1 / half
    d1a, d1b = q1 * q0 * d0 + step * r1a, step * r1b
    r2a = r1a - lam * d1a
    r2b = r1b - d1a - lam * d1b
    r2c = -d1b
    q2 = 1.0 / (2.0 * sig - q1)
    step = 2.0 * q2 / half
    d2a, d2b, d2c = q2 * q1 * d1a + step * r2a, q2 * q1 * d1b + step * r2b, step * r2c
    return d0 + d1a + d2a, d1b + d2b, d2c


def ridge_kernel(count, depth, lam, core, every, between, rhs_shift, slope, square, standard,
                 sent, own, gram, cross, weights, swapped):
    samp = every.shape[0]
    width, trait_count = gram.shape[0], cross.shape[0]
    gram_places, cross_places = places(width, trait_count, samp)
    for row, column, owned, place in gram_tiles(width, samp):
        gram[row : row + 8, column : column + TILE] = every[
            owned, :, place * TILE : (place + 1) * TILE
        ].astype(F32)
    for block_row in range(width // TILE):
        for block_column in range(block_row + 1, width // TILE):
            gram[block_column * TILE : (block_column + 1) * TILE, block_row * TILE : (block_row + 1) * TILE] = gram[
                block_row * TILE : (block_row + 1) * TILE, block_column * TILE : (block_column + 1) * TILE
            ].T
    for row, column, owned, place in cross_tiles(trait_count, width, samp):
        at = (gram_places + place) * TILE
        low = at + cross_places * TILE
        cross[row : row + 8, column : column + TILE] = every[owned, :, at : at + TILE].astype(F32) + every[
            owned, :, low : low + TILE
        ].astype(F32)
    scale = slope[...]
    diagonal = square[...]
    matrix = gram[...] * (1.0 / count) + between[...]
    same = lax.broadcasted_iota(jnp.int32, matrix.shape, 0) == lax.broadcasted_iota(jnp.int32, matrix.shape, 1)
    matrix = jnp.where(same, 0.0, matrix)
    rhs = cross[...] * (1.0 / count) * scale + rhs_shift[...]

    def apply_gram(values):
        return dot(values * scale, matrix, ((1,), (0,)), EXACT) * scale + diagonal * values

    once = apply_gram(rhs)
    twice = apply_gram(once)
    eight = jnp.broadcast_to(scale, (8, width))
    column_sums = dot(eight, jnp.abs(matrix), ((1,), (0,)), EXACT)[0:1] * scale + diagonal
    bound = jnp.max(column_sums, axis=1, keepdims=True)
    powers = [(v, swapped_tiles(v)) for v in (rhs, once, twice)]
    for r in range(RIDGE):
        coefficients = [
            jnp.broadcast_to(v, (8, width))
            for v in chebyshev_coefficients(jnp.full((1, 1), lam[r], F32), bound)
        ]
        for y in range(depth):
            at, to = slice(8 * y, 8 * y + 8), 8 * (RIDGE * y + r)
            for which, ref in enumerate((weights, swapped)):
                ref[to : to + 8] = sum(c * p[which][at] for c, p in zip(coefficients, powers))
    side = (lax.broadcasted_iota(jnp.int32, weights.shape, 0) >> 2) & 1
    mine = core[0]
    both = weights[...], swapped[...]
    own[...] = jnp.where(side == mine, *both).astype(BF16)
    sent[...] = halves(jnp.where(side == 1 - mine, *both).astype(BF16), standard)


def swapped_tiles(values):
    tiles = [jnp.roll(values[at : at + 8], 4, axis=0) for at in range(0, values.shape[0], 8)]
    return jnp.concatenate(tiles, axis=0)


def halves(weights, standard):
    half = standard.shape[0] // 2
    along = ((1,), (1,))
    first = dot(weights, standard[:half], along)
    second = dot(weights, standard[half:], along)
    low = (lax.broadcasted_iota(jnp.int32, first.shape, 0) & 4) == 0
    return jnp.where(low, first, second).astype(BF16)


def ridge(lam, core, every, between, rhs_shift, slope, square, standard, count, depth):
    rows, width = standard.shape
    trait_count = rhs_shift.shape[0]
    vmem, smem = pl.BlockSpec(memory_space=pltpu.VMEM), pl.BlockSpec(memory_space=pltpu.SMEM)
    return pl.pallas_call(
        functools.partial(ridge_kernel, count, depth),
        in_specs=[smem] * 2 + [vmem] * 6,
        out_specs=[vmem, vmem],
        out_shape=[
            jax.ShapeDtypeStruct((RIDGE * trait_count, rows // 2), BF16),
            jax.ShapeDtypeStruct((RIDGE * trait_count, width), BF16),
        ],
        scratch_shapes=[
            pltpu.VMEM((width, width), F32),
            pltpu.VMEM((trait_count, width), F32),
            pltpu.VMEM((RIDGE * trait_count, width), F32),
            pltpu.VMEM((RIDGE * trait_count, width), F32),
        ],
        compiler_params=pltpu.CompilerParams(vmem_limit_bytes=LIMIT),
        name="ridge",
    )(lam, core, every, between, rhs_shift, slope, square, standard)


def kept_kernel(weights, standard, out):
    out[...] = halves(weights[...], standard)


def kept_rows(weights, standard):
    vmem = pl.BlockSpec(memory_space=pltpu.VMEM)
    return pl.pallas_call(
        kept_kernel,
        in_specs=[vmem, vmem],
        out_specs=vmem,
        out_shape=jax.ShapeDtypeStruct((weights.shape[0], standard.shape[0] // 2), BF16),
        compiler_params=pltpu.CompilerParams(vmem_limit_bytes=LIMIT),
        name="kept",
    )(weights, standard)


def residual_kernel(summed, own_traits, out, out_bf, flat):
    pred = jnp.sum(summed[...].astype(F32), axis=0)
    _, rows = own_traits.shape
    half = rows // 2
    for r in range(RIDGE):
        for h in range(2):
            lanes = slice(h * half, (h + 1) * half)
            at = 8 * r + 4 * h
            value = own_traits[:, lanes] - pred[at : at + 4]
            out[r, :, lanes] = value
            flat[4 * r : 4 * r + 4, lanes] = value
    out_bf[0] = flat[...].astype(BF16)


def residuals(summed, own_traits):
    share, rows = own_traits.shape
    vmem = pl.BlockSpec(memory_space=pltpu.VMEM)
    return pl.pallas_call(
        residual_kernel,
        in_specs=[vmem, vmem],
        out_specs=[vmem, vmem],
        out_shape=[
            jax.ShapeDtypeStruct((RIDGE, share, rows), F32),
            jax.ShapeDtypeStruct((1, RIDGE * share, rows), BF16),
        ],
        scratch_shapes=[pltpu.VMEM((RIDGE * share, rows), F32)],
        compiler_params=pltpu.CompilerParams(vmem_limit_bytes=LIMIT),
        name="residuals",
    )(summed, own_traits)


def from_sums(sums, dosages, new_dosages, trait_count, count):
    (rows, width), samp = dosages.shape, sums.shape[0]
    code_sums = sums[:, :, :TILE].reshape(samp, width)
    trait_sums = sums[:, 2, 2 * TILE : 2 * TILE + trait_count]
    totals = jnp.sum(sums, axis=0)
    code_sum, code_sq = totals[:, :TILE].reshape(width), totals[:, TILE : 2 * TILE].reshape(width)
    new_sum, new_sq = totals[0, 2 * TILE :], totals[1, 2 * TILE :]
    trait_sum = totals[2, 2 * TILE : 2 * TILE + trait_count]
    mean, inv = column_stats(code_sum, code_sq, count)
    value_mean, slope, square = affine(code_sum, code_sq, mean, inv, count)
    new_mean, new_inv = column_stats(new_sum, new_sq, count)
    standard = scaled(dosages, mean, inv)
    fresh = scaled(new_dosages, new_mean, new_inv)
    code_shift = code_sums / rows - code_sum / count
    trait_shift = trait_sums / rows - trait_sum / count
    over_parts = ((0,), (0,))
    between = dot(code_shift, code_shift, over_parts, EXACT) * (1.0 / samp)
    rhs_shift = dot(trait_shift, code_shift, over_parts, EXACT) * (slope[None] * (1.0 / samp))
    rhs_shift = rhs_shift + (trait_sum / count)[:, None] * value_mean[None]
    return standard, fresh, between, rhs_shift, slope, square


def shards(dosages, new_dosages, traits, shrink):
    rows, width = dosages.shape
    fresh_width = new_dosages.shape[1]
    trait_count = traits.shape[0]
    samp, blk = lax.axis_size(SAMP), lax.axis_size(BLK)
    depth, xs, zs = lax.axis_size("y"), lax.axis_size("x"), lax.axis_size("z")
    count = float(rows * samp)
    share = trait_count // blk
    used = RIDGE * share
    padded = (used // 8 + 1) * 8
    gram_places, cross_places = places(width, trait_count, samp)

    payload = products(dosages, new_dosages, traits, samp)
    received = lax.all_to_all(payload, SAMP, 0, 0, tiled=True)
    own_rows, sums = owner(received, gram_places * TILE, cross_places * TILE)
    every = lax.all_to_all(own_rows, SAMP, 0, 0, tiled=True)
    prepared = from_sums(sums, dosages, new_dosages, trait_count, count)
    standard, fresh, between, rhs_shift, slope, square = prepared

    core = lax.axis_index("core").astype(jnp.int32).reshape(1)
    sent, own = ridge(
        shrink, core, every, between, rhs_shift, slope[None], square[None], standard, count, depth
    )

    arrived = lax.ppermute(sent, "core", [(0, 1), (1, 0)])
    kept = kept_rows(own, standard)
    paired = (kept.astype(F32) + arrived.astype(F32)).astype(BF16)
    summed = lax.all_to_all(
        paired.reshape(depth, paired.shape[0] // depth, rows // 2), "y", 0, 0, tiled=True
    )
    own_traits = lax.dynamic_slice_in_dim(traits, lax.axis_index(BLK) * share, share, 0)
    residual, res_bf = residuals(summed, own_traits)
    res_bf = lax.all_gather(res_bf, BLK, axis=0, tiled=True)
    res_bf = res_bf.reshape(blk * used, rows)
    raw_part = dot(res_bf, fresh, ((1,), (0,))).reshape(blk, used, fresh_width)
    res_float = res_bf.astype(F32)
    squares = jnp.sum(res_float * res_float, axis=1).reshape(blk, 1, used)
    squares = jnp.pad(squares, ((0, 0), (0, padded - used - 1), (0, fresh_width - used)))
    ends = jnp.concatenate([raw_part, squares], axis=1)
    ends = lax.all_to_all(ends.reshape(zs, blk // zs * padded, fresh_width), "z", 0, 0, tiled=True)
    ends = jnp.sum(ends, axis=0)
    ends = lax.all_to_all(jnp.broadcast_to(ends[None], (xs, *ends.shape)), "x", 0, 0, tiled=True)
    ends = jnp.sum(ends, axis=0).reshape(blk // zs, padded, fresh_width)
    sum_sq = ends[:, used, :used]
    scores = ends[:, :used] / jnp.sqrt(count * (sum_sq / count + EPS))[:, :, None]
    scores = scores.reshape(blk // zs * used, fresh_width).astype(BF16)
    scores = lax.all_to_all(
        jnp.broadcast_to(scores[None], (zs, *scores.shape)), "z", 0, 0, tiled=True
    )
    scores = scores.astype(F32).reshape(blk, RIDGE, share, fresh_width).transpose(1, 0, 2, 3)
    return residual, scores.reshape(RIDGE, trait_count, fresh_width)


def solution(mesh):
    samp, blk = FACTORS[mesh.shape["samp"]], FACTORS[mesh.shape["blk"]]
    grid = Mesh(mesh.devices.reshape(*samp, *blk), SAMP + BLK)
    return jax.shard_map(
        shards,
        mesh=grid,
        in_specs=(P(SAMP, BLK), P(SAMP, BLK), P(None, SAMP), P()),
        out_specs=(P(None, BLK, SAMP), P(None, None, BLK)),
        check_vma=False,
    )
```

```python
import functools

import jax
import jax.numpy as jnp
from jax import lax
from jax.experimental import pallas as pl
from jax.experimental.pallas import tpu as pltpu
from jax.sharding import Mesh, PartitionSpec as P


RIDGE = 5
SAMP = ("x", "z")
BLK = ("y", "core")
FACTORS = {32: (4, 8), 16: (8, 2), 4: (2, 2)}
EPS = 1e-05
TILE = 128
SUMS = 3 * TILE
F32 = jnp.float32
BF16 = jnp.bfloat16
LIMIT = 30 << 20
EXACT = lax.Precision.HIGHEST


def dot(a, b, contract, precision=None):
    return lax.dot_general(
        a, b, (contract, ((), ())), precision=precision, preferred_element_type=F32
    )


def rounded(values):
    return lax.reduce_precision(values, 8, 7)


def split(values):
    high = values.astype(BF16)
    return high, (values - high.astype(F32)).astype(BF16)


def gram_tiles(width, samp):
    at = 0
    for block_row in range(width // TILE):
        for block_column in range(block_row, width // TILE):
            for group in range(TILE // 8):
                yield block_row * TILE + 8 * group, block_column * TILE, at % samp, at // samp
                at += 1


def cross_tiles(trait_count, width, samp):
    at = 0
    for group in range(trait_count // 8):
        for block in range(width // TILE):
            yield 8 * group, block * TILE, at % samp, at // samp
            at += 1


def places(width, trait_count, samp):
    blocks = width // TILE
    gram = blocks * (blocks + 1) // 2 * (TILE // 8) // samp
    return gram, trait_count // 8 * blocks // samp


def products_kernel(samp, rows, dosages, new_dosages, traits, out, gram, cross, sums, new_sums, trait_sums):
    width, trait_count = dosages.shape[1], traits.shape[0]
    half = width // 2
    step = pl.program_id(0)

    @pl.when(step == 0)
    def _():
        for ref in (gram, cross, sums, new_sums, trait_sums):
            ref[...] = jnp.zeros_like(ref)

    codes_f = (dosages[...] - 1).astype(F32)
    codes = codes_f.astype(BF16)
    new_f = (new_dosages[...] - 1).astype(F32)
    trait_bf = traits[...].astype(BF16)
    ones = jnp.ones((8, codes.shape[0]), BF16)
    over_rows = ((0,), (0,))
    gram[:half, :] += dot(codes[:, :half], codes, over_rows)
    gram[half:, half:] += dot(codes[:, half:], codes[:, half:], over_rows)
    cross[...] += dot(trait_bf, codes, ((1,), (0,)))
    sums[:8] += dot(ones, codes, ((1,), (0,)))
    sums[8:] += dot(ones, (codes_f * codes_f).astype(BF16), ((1,), (0,)))
    new_sums[:8] += dot(ones, new_f.astype(BF16), ((1,), (0,)))
    new_sums[8:] += dot(ones, (new_f * new_f).astype(BF16), ((1,), (0,)))
    trait_sums[...] += dot(ones, trait_bf, ((1,), (1,)))

    @pl.when(step == pl.num_programs(0) - 1)
    def _():
        shift = 1.0 / rows
        local, line = sums[:8], lax.broadcasted_iota(jnp.int32, (8, width), 0)
        high = rounded_in_kernel(local)
        left = jnp.where(line < 4, jnp.where((line & 1) == 0, high, local - high), 0.0).astype(BF16)
        right = jnp.where(line < 2, high, local - high).astype(BF16)
        gram[:half, :] = gram[:half, :] - dot(left[:, :half], right, over_rows) * shift
        gram[half:, half:] = gram[half:, half:] - dot(left[:, half:], right[:, half:], over_rows) * shift
        top = rounded_in_kernel(trait_sums[...])
        middle = rounded_in_kernel(trait_sums[...] - top)
        bottom = trait_sums[...] - top - middle
        spot = lax.broadcasted_iota(jnp.int32, top.shape, 0)
        left = jnp.where((spot == 0) | (spot == 3), top, jnp.where((spot == 1) | (spot == 4), middle, bottom))
        left = jnp.where(spot < 6, left, 0.0).astype(BF16)
        right = jnp.where(line < 3, high, local - high).astype(BF16)
        cross[...] = cross[...] - dot(left, right, over_rows) * shift
        gram_places, cross_places = places(width, trait_count, samp)
        for row, column, owner, place in gram_tiles(width, samp):
            out[owner, :, place * TILE : (place + 1) * TILE] = gram[
                row : row + 8, column : column + TILE
            ].astype(BF16)
        for row, column, owner, place in cross_tiles(trait_count, width, samp):
            high, low = split(cross[row : row + 8, column : column + TILE])
            at = (gram_places + place) * TILE
            out[owner, :, at : at + TILE] = high
            at += cross_places * TILE
            out[owner, :, at : at + TILE] = low
        lines = []
        for block in range(4):
            line = [sums[0:1, block * TILE : (block + 1) * TILE], sums[8:9, block * TILE : (block + 1) * TILE]]
            if block == 0:
                line.append(new_sums[0:1])
            elif block == 1:
                line.append(new_sums[8:9])
            elif block == 2:
                spare = jnp.zeros((1, TILE - trait_count), F32)
                line.append(jnp.concatenate([trait_sums[0:1], spare], axis=1))
            else:
                line.append(jnp.zeros((1, TILE), F32))
            lines.append(jnp.concatenate(line, axis=1))
        values = jnp.concatenate(lines, axis=0)
        kept = rounded_in_kernel(values)
        packed = jnp.concatenate([kept, values - kept], axis=0).astype(BF16)
        at = (gram_places + 2 * cross_places) * TILE
        out[:, :, at:] = jnp.broadcast_to(packed[None], (samp, 8, SUMS))


def rounded_in_kernel(values):
    return values.astype(BF16).astype(F32)


def products(dosages, new_dosages, traits, samp):
    rows, width = dosages.shape
    fresh_width, trait_count = new_dosages.shape[1], traits.shape[0]
    gram_places, cross_places = places(width, trait_count, samp)
    lanes = (gram_places + 2 * cross_places) * TILE + SUMS
    step = min(512, rows)
    return pl.pallas_call(
        functools.partial(products_kernel, samp, rows),
        grid=(rows // step,),
        in_specs=[
            pl.BlockSpec((step, width), lambda i: (i, 0)),
            pl.BlockSpec((step, fresh_width), lambda i: (i, 0)),
            pl.BlockSpec((trait_count, step), lambda i: (0, i)),
        ],
        out_specs=pl.BlockSpec((samp, 8, lanes), lambda i: (0, 0, 0)),
        out_shape=jax.ShapeDtypeStruct((samp, 8, lanes), BF16),
        scratch_shapes=[
            pltpu.VMEM((width, width), F32),
            pltpu.VMEM((trait_count, width), F32),
            pltpu.VMEM((16, width), F32),
            pltpu.VMEM((16, fresh_width), F32),
            pltpu.VMEM((8, trait_count), F32),
        ],
        name="products",
    )(dosages, new_dosages, traits)


def owner_kernel(gram_lanes, cross_lanes, received, out, sums):
    samp = received.shape[0]
    values = received[:, :, gram_lanes + 2 * cross_lanes :].astype(F32)
    sums[...] = values[:, :4] + values[:, 4:]
    total = jnp.sum(received[:, :, : gram_lanes + 2 * cross_lanes].astype(F32), axis=0)
    cross = total[:, gram_lanes : gram_lanes + cross_lanes] + total[:, gram_lanes + cross_lanes :]
    high = rounded_in_kernel(cross)
    own = jnp.concatenate([total[:, :gram_lanes], high, cross - high], axis=1).astype(BF16)
    out[...] = jnp.broadcast_to(own[None], (samp, *own.shape))


def owner(received, gram_lanes, cross_lanes):
    lanes = gram_lanes + 2 * cross_lanes
    return pl.pallas_call(
        functools.partial(owner_kernel, gram_lanes, cross_lanes),
        out_shape=[
            jax.ShapeDtypeStruct((*received.shape[:2], lanes), BF16),
            jax.ShapeDtypeStruct((received.shape[0], 4, SUMS), F32),
        ],
        compiler_params=pltpu.CompilerParams(vmem_limit_bytes=LIMIT),
        name="owner",
    )(received)


def column_stats(shifted_sum, shifted_sq, count):
    mean = (shifted_sum + count) / count
    var = (shifted_sq + 2.0 * shifted_sum + count) / count - mean * mean
    return mean, 1.0 / jnp.sqrt(var + EPS)


def scaled(codes, mean, inv):
    return ((codes.astype(F32) - mean) * inv).astype(BF16)


def affine(shifted_sum, shifted_sq, mean, inv, count):
    low, mid, high = (rounded((code - mean) * inv) for code in (0.0, 1.0, 2.0))
    n_low = (shifted_sq - shifted_sum) * 0.5
    n_high = (shifted_sq + shifted_sum) * 0.5
    n_mid = count - shifted_sq
    value_mean = (n_low * low + n_mid * mid + n_high * high) / count
    pairs = n_low * n_mid + n_mid * n_high + 4.0 * n_low * n_high
    slopes = (
        n_low * n_mid * (mid - low)
        + n_mid * n_high * (high - mid)
        + 2.0 * n_low * n_high * (high - low)
    )
    slope = jnp.where(pairs > 0.0, slopes / jnp.maximum(pairs, 1.0), inv)
    square = (n_low * low * low + n_mid * mid * mid + n_high * high * high) / count
    return value_mean, slope, square


def chebyshev_coefficients(lam, bound):
    centre = lam + bound / 2.0
    half = bound / 2.0
    sig = centre / half
    q0 = 1.0 / sig
    d0 = 1.0 / centre
    r1a, r1b = 1.0 - lam * d0, -d0
    q1 = 1.0 / (2.0 * sig - q0)
    step = 2.0 * q1 / half
    d1a, d1b = q1 * q0 * d0 + step * r1a, step * r1b
    r2a = r1a - lam * d1a
    r2b = r1b - d1a - lam * d1b
    r2c = -d1b
    q2 = 1.0 / (2.0 * sig - q1)
    step = 2.0 * q2 / half
    d2a, d2b, d2c = q2 * q1 * d1a + step * r2a, q2 * q1 * d1b + step * r2b, step * r2c
    return d0 + d1a + d2a, d1b + d2b, d2c


def ridge_kernel(count, depth, lam, core, every, between, rhs_shift, slope, square, standard,
                 sent, own, gram, cross, weights, swapped):
    samp = every.shape[0]
    width, trait_count = gram.shape[0], cross.shape[0]
    gram_places, cross_places = places(width, trait_count, samp)
    for row, column, owned, place in gram_tiles(width, samp):
        gram[row : row + 8, column : column + TILE] = every[
            owned, :, place * TILE : (place + 1) * TILE
        ].astype(F32)
    for block_row in range(width // TILE):
        for block_column in range(block_row + 1, width // TILE):
            gram[block_column * TILE : (block_column + 1) * TILE, block_row * TILE : (block_row + 1) * TILE] = gram[
                block_row * TILE : (block_row + 1) * TILE, block_column * TILE : (block_column + 1) * TILE
            ].T
    for row, column, owned, place in cross_tiles(trait_count, width, samp):
        at = (gram_places + place) * TILE
        low = at + cross_places * TILE
        cross[row : row + 8, column : column + TILE] = every[owned, :, at : at + TILE].astype(F32) + every[
            owned, :, low : low + TILE
        ].astype(F32)
    scale = slope[...]
    diagonal = square[...]
    matrix = gram[...] * (1.0 / count) + between[...]
    same = lax.broadcasted_iota(jnp.int32, matrix.shape, 0) == lax.broadcasted_iota(jnp.int32, matrix.shape, 1)
    matrix = jnp.where(same, 0.0, matrix)
    rhs = cross[...] * (1.0 / count) * scale + rhs_shift[...]

    parts, sizes = split(matrix), split(jnp.abs(matrix))

    def product(values, high, low):
        count = values.shape[0]
        top, bottom = split(values)
        out = dot(jnp.concatenate([top, bottom], axis=0), high, ((1,), (0,)))
        return out[:count] + out[count:] + dot(top, low, ((1,), (0,)))

    def apply_gram(values):
        return product(values * scale, *parts) * scale + diagonal * values

    once = apply_gram(rhs)
    twice = apply_gram(once)
    eight = jnp.broadcast_to(scale, (8, width))
    column_sums = product(eight, *sizes)[0:1] * scale + diagonal
    bound = jnp.max(column_sums, axis=1, keepdims=True)
    powers = [(v, swapped_tiles(v)) for v in (rhs, once, twice)]
    for r in range(RIDGE):
        coefficients = [
            jnp.broadcast_to(v, (8, width))
            for v in chebyshev_coefficients(jnp.full((1, 1), lam[r], F32), bound)
        ]
        for y in range(depth):
            at, to = slice(8 * y, 8 * y + 8), 8 * (RIDGE * y + r)
            for which, ref in enumerate((weights, swapped)):
                ref[to : to + 8] = sum(c * p[which][at] for c, p in zip(coefficients, powers))
    side = (lax.broadcasted_iota(jnp.int32, weights.shape, 0) >> 2) & 1
    mine = core[0]
    both = weights[...], swapped[...]
    own[...] = jnp.where(side == mine, *both).astype(BF16)
    sent[...] = halves(jnp.where(side == 1 - mine, *both).astype(BF16), standard)


def swapped_tiles(values):
    tiles = [jnp.roll(values[at : at + 8], 4, axis=0) for at in range(0, values.shape[0], 8)]
    return jnp.concatenate(tiles, axis=0)


def halves(weights, standard):
    half = standard.shape[0] // 2
    along = ((1,), (1,))
    first = dot(weights, standard[:half], along)
    second = dot(weights, standard[half:], along)
    low = (lax.broadcasted_iota(jnp.int32, first.shape, 0) & 4) == 0
    return jnp.where(low, first, second).astype(BF16)


def ridge(lam, core, every, between, rhs_shift, slope, square, standard, count, depth):
    rows, width = standard.shape
    trait_count = rhs_shift.shape[0]
    vmem, smem = pl.BlockSpec(memory_space=pltpu.VMEM), pl.BlockSpec(memory_space=pltpu.SMEM)
    return pl.pallas_call(
        functools.partial(ridge_kernel, count, depth),
        in_specs=[smem] * 2 + [vmem] * 6,
        out_specs=[vmem, vmem],
        out_shape=[
            jax.ShapeDtypeStruct((RIDGE * trait_count, rows // 2), BF16),
            jax.ShapeDtypeStruct((RIDGE * trait_count, width), BF16),
        ],
        scratch_shapes=[
            pltpu.VMEM((width, width), F32),
            pltpu.VMEM((trait_count, width), F32),
            pltpu.VMEM((RIDGE * trait_count, width), F32),
            pltpu.VMEM((RIDGE * trait_count, width), F32),
        ],
        compiler_params=pltpu.CompilerParams(vmem_limit_bytes=LIMIT),
        name="ridge",
    )(lam, core, every, between, rhs_shift, slope, square, standard)


def kept_kernel(weights, standard, out):
    out[...] = halves(weights[...], standard)


def kept_rows(weights, standard):
    vmem = pl.BlockSpec(memory_space=pltpu.VMEM)
    return pl.pallas_call(
        kept_kernel,
        in_specs=[vmem, vmem],
        out_specs=vmem,
        out_shape=jax.ShapeDtypeStruct((weights.shape[0], standard.shape[0] // 2), BF16),
        compiler_params=pltpu.CompilerParams(vmem_limit_bytes=LIMIT),
        name="kept",
    )(weights, standard)


def residual_kernel(summed, own_traits, out, out_bf, flat):
    pred = jnp.sum(summed[...].astype(F32), axis=0)
    _, rows = own_traits.shape
    half = rows // 2
    for r in range(RIDGE):
        for h in range(2):
            lanes = slice(h * half, (h + 1) * half)
            at = 8 * r + 4 * h
            value = own_traits[:, lanes] - pred[at : at + 4]
            out[r, :, lanes] = value
            flat[4 * r : 4 * r + 4, lanes] = value
    out_bf[0] = flat[...].astype(BF16)


def residuals(summed, own_traits):
    share, rows = own_traits.shape
    vmem = pl.BlockSpec(memory_space=pltpu.VMEM)
    return pl.pallas_call(
        residual_kernel,
        in_specs=[vmem, vmem],
        out_specs=[vmem, vmem],
        out_shape=[
            jax.ShapeDtypeStruct((RIDGE, share, rows), F32),
            jax.ShapeDtypeStruct((1, RIDGE * share, rows), BF16),
        ],
        scratch_shapes=[pltpu.VMEM((RIDGE * share, rows), F32)],
        compiler_params=pltpu.CompilerParams(vmem_limit_bytes=LIMIT),
        name="residuals",
    )(summed, own_traits)


def from_sums(sums, dosages, new_dosages, trait_count, count):
    (rows, width), samp = dosages.shape, sums.shape[0]
    code_sums = sums[:, :, :TILE].reshape(samp, width)
    trait_sums = sums[:, 2, 2 * TILE : 2 * TILE + trait_count]
    totals = jnp.sum(sums, axis=0)
    code_sum, code_sq = totals[:, :TILE].reshape(width), totals[:, TILE : 2 * TILE].reshape(width)
    new_sum, new_sq = totals[0, 2 * TILE :], totals[1, 2 * TILE :]
    trait_sum = totals[2, 2 * TILE : 2 * TILE + trait_count]
    mean, inv = column_stats(code_sum, code_sq, count)
    value_mean, slope, square = affine(code_sum, code_sq, mean, inv, count)
    new_mean, new_inv = column_stats(new_sum, new_sq, count)
    standard = scaled(dosages, mean, inv)
    fresh = scaled(new_dosages, new_mean, new_inv)
    code_shift = code_sums / rows - code_sum / count
    trait_shift = trait_sums / rows - trait_sum / count
    over_parts = ((0,), (0,))
    between = dot(code_shift, code_shift, over_parts, EXACT) * (1.0 / samp)
    rhs_shift = dot(trait_shift, code_shift, over_parts, EXACT) * (slope[None] * (1.0 / samp))
    rhs_shift = rhs_shift + (trait_sum / count)[:, None] * value_mean[None]
    return standard, fresh, between, rhs_shift, slope, square


def shards(dosages, new_dosages, traits, shrink):
    rows, width = dosages.shape
    fresh_width = new_dosages.shape[1]
    trait_count = traits.shape[0]
    samp, blk = lax.axis_size(SAMP), lax.axis_size(BLK)
    depth, xs, zs = lax.axis_size("y"), lax.axis_size("x"), lax.axis_size("z")
    count = float(rows * samp)
    share = trait_count // blk
    used = RIDGE * share
    padded = (used // 8 + 1) * 8
    gram_places, cross_places = places(width, trait_count, samp)

    payload = products(dosages, new_dosages, traits, samp)
    received = lax.all_to_all(payload, SAMP, 0, 0, tiled=True)
    own_rows, sums = owner(received, gram_places * TILE, cross_places * TILE)
    every = lax.all_to_all(own_rows, SAMP, 0, 0, tiled=True)
    prepared = from_sums(sums, dosages, new_dosages, trait_count, count)
    standard, fresh, between, rhs_shift, slope, square = prepared

    core = lax.axis_index("core").astype(jnp.int32).reshape(1)
    sent, own = ridge(
        shrink, core, every, between, rhs_shift, slope[None], square[None], standard, count, depth
    )

    arrived = lax.ppermute(sent, "core", [(0, 1), (1, 0)])
    kept = kept_rows(own, standard)
    paired = (kept.astype(F32) + arrived.astype(F32)).astype(BF16)
    summed = lax.all_to_all(
        paired.reshape(depth, paired.shape[0] // depth, rows // 2), "y", 0, 0, tiled=True
    )
    own_traits = lax.dynamic_slice_in_dim(traits, lax.axis_index(BLK) * share, share, 0)
    residual, res_bf = residuals(summed, own_traits)
    res_bf = lax.all_gather(res_bf, BLK, axis=0, tiled=True)
    res_bf = res_bf.reshape(blk * used, rows)
    raw_part = dot(res_bf, fresh, ((1,), (0,))).reshape(blk, used, fresh_width)
    res_float = res_bf.astype(F32)
    squares = jnp.sum(res_float * res_float, axis=1).reshape(blk, 1, used)
    squares = jnp.pad(squares, ((0, 0), (0, padded - used - 1), (0, fresh_width - used)))
    ends = jnp.concatenate([raw_part, squares], axis=1)
    ends = lax.all_to_all(ends.reshape(zs, blk // zs * padded, fresh_width), "z", 0, 0, tiled=True)
    ends = jnp.sum(ends, axis=0)
    ends = lax.all_to_all(jnp.broadcast_to(ends[None], (xs, *ends.shape)), "x", 0, 0, tiled=True)
    ends = jnp.sum(ends, axis=0).reshape(blk // zs, padded, fresh_width)
    sum_sq = ends[:, used, :used]
    scores = ends[:, :used] / jnp.sqrt(count * (sum_sq / count + EPS))[:, :, None]
    scores = scores.reshape(blk // zs * used, fresh_width).astype(BF16)
    scores = lax.all_to_all(
        jnp.broadcast_to(scores[None], (zs, *scores.shape)), "z", 0, 0, tiled=True
    )
    scores = scores.astype(F32).reshape(blk, RIDGE, share, fresh_width).transpose(1, 0, 2, 3)
    return residual, scores.reshape(RIDGE, trait_count, fresh_width)


def solution(mesh):
    samp, blk = FACTORS[mesh.shape["samp"]], FACTORS[mesh.shape["blk"]]
    grid = Mesh(mesh.devices.reshape(*samp, *blk), SAMP + BLK)
    return jax.shard_map(
        shards,
        mesh=grid,
        in_specs=(P(SAMP, BLK), P(SAMP, BLK), P(None, SAMP), P()),
        out_specs=(P(None, BLK, SAMP), P(None, None, BLK)),
        check_vma=False,
    )
```
